32 devices in a mesh: grp: 2 (over y), dp: 16 (over z, x, core).
Axes of the slice: x: 2, y: 2, z: 4, core: 2. Of those that a mesh axis runs over, the one named last changes fastest.
Arguments:
- query_act: bfloat16 [32768, 256], P(('grp', 'dp')), parts along dimension 0, may hold values from -6 to 6
- query_grad: bfloat16 [32768, 256], P(('grp', 'dp')), parts along dimension 0, may hold values from -6 to 6
- train_act: bfloat16 [32, 64, 256], P(('grp', 'dp')), parts along dimension 0, may hold values from -12 to 12
- train_grad: bfloat16 [32, 64, 256], P(('grp', 'dp')), parts along dimension 0, may hold values from -12 to 12
- seq_ids: int32 [32, 64], P(('grp', 'dp')), parts along dimension 0, may hold values from 0 to 3, never falling along the last dimension, each value on 1 to 32 neighbouring positions
Outputs:
- scores: float32 [32768, 64], P(('grp', 'dp')), parts along dimension 0
The draws below stay inside these ranges and needn't reach their ends.
There are 2 independent parts, one for each index of `grp`. The reference program is written for one: setup_inputs(seed, part) draws one part's arguments, and reference() takes and returns one part's arrays. A program takes and returns all parts, laid end to end along the dimension named above; each array names one. Nothing has to cross between parts.
Inputs may be any that keep to these rules, and one draw needn't show every extreme that they name: `seq_ids`: within a span the ids never fall and each of the 4 sequences holds 1 to 32 tokens, one exactly 32.
All inputs are finite; a program needn't handle non-finite values.
Results may differ from the reference program's by a relative error of at most 0.023.
The reference program's roundings to bfloat16 on the way count: a program that leaves them out, or rounds other values in their place, can miss the bound.
Values may be sent and summed in bfloat16 or wider, within the bound.
No kernel may reach another device: no remote copies, remote signals or barrier semaphores. Data moves between devices by JAX's collectives and lax.ppermute only.
A program may use at most 192 MiB of HBM per device.

```python
import math
import jax
import jax.numpy as jnp
import numpy as np
from jax import lax

RA = 256
RG = 256
C_DEV = 64
SEQ_DEV = 4
QUERIES = 16384
N_DP = 16


def spread_features(key, width):
    key_scale, key_noise, key_mixing, key_directions = jax.random.split(key, 4)
    shape = (N_DP, C_DEV, width)
    column_scales = jnp.exp(jax.random.uniform(key_scale, (width,), jnp.float32, math.log(0.03), math.log(3.0)))
    noise_part = jax.random.normal(key_noise, shape, jnp.float32)
    amplitude = 0.75
    mixing = jax.random.normal(key_mixing, (N_DP, C_DEV, 4), jnp.float32)
    directions = jax.random.normal(key_directions, (4, width), jnp.float32)
    shared = mixing[:, :, 0:1] * directions[0][None, None, :]
    for component in range(1, 4):
        shared = shared + mixing[:, :, component:component + 1] * directions[component][None, None, :]
    values = noise_part * column_scales[None, None, :] + amplitude * shared
    return jnp.clip(values, -12.0, 12.0)


def draw_train_act(key, part):
    return spread_features(jax.random.fold_in(key, 11), RA).astype(jnp.bfloat16)


def draw_train_grad(key, part):
    return spread_features(jax.random.fold_in(key, 23), RG).astype(jnp.bfloat16)


def steps_of(key, dims, cuts, low, largest):
    gain = 1.0
    for position, parts in cuts:
        steps = jax.random.uniform(jax.random.fold_in(jax.random.fold_in(key, 6), position), (parts,), jnp.float32, low / len(cuts), largest / len(cuts))
        gain = gain * jnp.repeat(jnp.exp(steps), dims[position] // parts).reshape((-1,) + (1,) * (len(dims) - 1 - position))
    return gain


def profile(count, total, bound, slope):
    portions = [(1 << 20) // math.isqrt(grade ** slope) + 1 for grade in range(2, count + 1)]
    surplus, holding = total - bound - (count - 1), [1] * (count - 1)
    while surplus > 0:
        candidates = [i for i in range(count - 1) if holding[i] < bound]
        whole, remaining = sum([portions[i] for i in candidates]), surplus
        for i in candidates:
            addition = min(bound - holding[i], max(1, remaining * portions[i] // whole), surplus)
            holding[i] = holding[i] + addition
            surplus = surplus - addition
    return np.array([bound] + holding)


def ragged(rng, amount, total, bound, lean):
    if amount == 2:
        one = jax.random.randint(rng, (), max(1, total - bound), min(bound, total - 1) + 1)
        return jnp.stack([one, total - one])
    lengths = jnp.asarray(profile(amount, total, bound, lean), jnp.int32)
    twos = (amount - 1) // 2
    source_of, sink = lengths[1:1 + 2 * twos:2], lengths[2:2 + 2 * twos:2]
    room = jnp.minimum(source_of - 1, bound - sink)
    moved = jax.random.randint(jax.random.fold_in(rng, 1), (twos,), 0, 1 << 20) % (room + 1)
    lengths = lengths.at[1:1 + 2 * twos:2].set(source_of - moved).at[2:2 + 2 * twos:2].set(sink + moved)
    return lengths[jax.random.permutation(jax.random.fold_in(rng, 2), amount)]


def normal_values(stream_key, shape, deviation, reach, shards=(), held_as=jnp.bfloat16):
    entries = deviation * jax.random.normal(stream_key, shape, jnp.float32)
    if shards:
        entries = entries * steps_of(stream_key, shape, shards, -0.22, 0.18)
    return jnp.clip(entries, -reach, reach).astype(held_as)


def setup_inputs(seed: int = 0, part: int = 0) -> dict:
    keys = jax.random.split(jax.random.key(seed), 6)
    part_splits = jax.random.split(jax.random.fold_in(keys[5], part), 6)
    return {
        "query_act": normal_values(part_splits[0], (QUERIES, RA), 1.0, 6.0, ((0, 16),)),
        "query_grad": normal_values(part_splits[1], (QUERIES, RG), 1.0, 6.0, ((0, 16),)),
        "train_act": draw_train_act(jax.random.fold_in(jax.random.fold_in(keys[5], part), 71), part),
        "train_grad": draw_train_grad(jax.random.fold_in(jax.random.fold_in(keys[5], part), 71), part),
        "seq_ids": jax.vmap(lambda own: jnp.searchsorted(jnp.cumsum(ragged(own, SEQ_DEV, C_DEV, C_DEV // 2, 0)), jnp.arange(C_DEV), side="right"))(jax.random.split(part_splits[4], N_DP)).reshape((N_DP, C_DEV)).astype(jnp.int32),
    }


damping = 0.1

def precondition(queries, train):
    flat = train.reshape(-1, train.shape[-1])
    covar = jnp.dot(flat.T.astype(jnp.float32), flat.astype(jnp.float32), preferred_element_type=jnp.float32)
    width = train.shape[-1]
    matrix = covar / flat.shape[0] + damping * jnp.eye(width, dtype=jnp.float32)
    factor = jnp.linalg.cholesky(matrix)
    solved = jax.scipy.linalg.cho_solve((factor, True), queries.astype(jnp.float32).T)
    return solved.T.astype(jnp.bfloat16)

def reference(query_act, query_grad, train_act, train_grad, seq_ids):
    query_pa = precondition(query_act, train_act)
    query_pg = precondition(query_grad, train_grad)
    scale = 1.0 / (8.0 * math.sqrt(query_act.shape[1] * query_grad.shape[1]))

    def one_span(inputs):
        act_rows, grad_rows, seg_rows = inputs
        gram_a = jnp.dot(query_pa.astype(jnp.float32), act_rows.T.astype(jnp.float32), preferred_element_type=jnp.float32)
        gram_g = jnp.dot(query_pg.astype(jnp.float32), grad_rows.T.astype(jnp.float32), preferred_element_type=jnp.float32)
        product = gram_a * gram_g
        onehot = (seg_rows[:, None] == jnp.arange(SEQ_DEV, dtype=jnp.int32)[None, :]).astype(jnp.float32)
        return jnp.dot(product.astype(jnp.float32), onehot.astype(jnp.float32), precision=lax.Precision.HIGHEST, preferred_element_type=jnp.float32) * scale
    blocks = lax.map(one_span, (train_act, train_grad, seq_ids))
    return jnp.transpose(blocks, (1, 0, 2)).reshape(blocks.shape[1], -1)
```

```python
import math

import jax
import jax.numpy as jnp
from jax import lax
from jax.experimental import pallas as pl
from jax.experimental.pallas import tpu as pltpu
from jax.sharding import PartitionSpec as P

SEQ_DEV = 4
DAMPING = 0.1

BF16 = jnp.bfloat16
F32 = jnp.float32


def newton_schedule():
    radius, bounds, scales = 3e-3, [], []
    for _ in range(13):
        before = math.sqrt(2.0 * radius / (1.0 + radius))
        scales.append(2.0 / (2.0 - before * before))
        bounds.append(2.0 * DAMPING / (1.0 - before) - DAMPING)
        radius = before
    return bounds, scales


BOUNDS, SCALES = newton_schedule()


def pick(index, values):
    out = jnp.float32(values[0])
    for position, value in enumerate(values[1:], 2):
        out = jnp.where(index == position, jnp.float32(value), out)
    return out


def split2(x):
    high = x.astype(BF16)
    return high, (x - high.astype(F32)).astype(BF16)


def split3(x):
    high = x.astype(BF16)
    rest = x - high.astype(F32)
    mid = rest.astype(BF16)
    return high, mid, (rest - mid.astype(F32)).astype(BF16)


def dot(a, b):
    return jnp.dot(a, b, preferred_element_type=F32)


def dot3(a, b):
    return dot(a[0], b[0]) + (dot(a[0], b[1]) + dot(a[1], b[0]))


def dot6(a, b):
    small = dot(a[1], b[1]) + (dot(a[0], b[2]) + dot(a[2], b[0]))
    return dot(a[0], b[0]) + ((dot(a[0], b[1]) + dot(a[1], b[0])) + small)


def dot_nt(a, b):
    return lax.dot_general(a, b, (((1,), (1,)), ((), ())), preferred_element_type=F32)


def influence_kernel(rows, scale, *refs):
    n_pieces = len(refs) - 10
    pieces = refs[:n_pieces]
    query_act, query_grad, out, act, grad, onehot, mat, tmat, xmat, inverse = refs[n_pieces:]
    tokens, width = act.shape
    columns = onehot.shape[0]
    lane = lax.broadcasted_iota(jnp.int32, (1, 128), 1)
    column = lax.broadcasted_iota(jnp.int32, (columns, 128), 0)

    spans = [(ref, k) for ref in pieces for k in range(ref.shape[0])]
    labels = []
    for slot, (ref, k) in enumerate(spans):
        act[slot * rows : (slot + 1) * rows, :] = ref[k, 0:rows, :]
        grad[slot * rows : (slot + 1) * rows, :] = ref[k, rows : 2 * rows, :]
        tail = ref[k, 2 * rows : 2 * rows + 16, 0:128].astype(F32)
        labels.append((SEQ_DEV * tail[1:2, :] + tail[0:1, :]).astype(jnp.int32))
    for pair in range(tokens // 128):
        label = jnp.where(lane < rows, labels[2 * pair], labels[2 * pair + 1])
        onehot[:, pair * 128 : (pair + 1) * 128] = (column == label).astype(F32).astype(BF16)

    diagonal = lax.broadcasted_iota(jnp.int32, (width, width), 0) == lax.broadcasted_iota(jnp.int32, (width, width), 1)
    eye = diagonal.astype(F32)
    norm = jnp.float32(0.0)
    for which, features in enumerate((act, grad)):
        flat = features[...]
        covar = lax.dot_general(flat, flat, (((0,), (0,)), ((), ())), preferred_element_type=F32)
        matrix = covar * (1.0 / tokens) + DAMPING * eye
        mat[which] = matrix
        norm = jnp.maximum(norm, jnp.sum(matrix * matrix))

    steps = jnp.int32(2)
    for bound in BOUNDS[1:-1]:
        steps = steps + (norm > bound * bound).astype(jnp.int32)
    start = pick(steps, [2.0 / (DAMPING + bound) for bound in BOUNDS])

    first = pick(steps, SCALES)
    for which in range(2):
        t = start * mat[which]
        parts = split2(t)
        xmat[which] = (first * start) * (2.0 * eye - t)
        tmat[which] = first * (2.0 * t - dot3(parts, parts))

    def step(i, carry):
        factor = pick(steps - i, SCALES)
        for which in range(2):
            t, x = tmat[which], xmat[which]
            tparts, xparts = split2(t), split2(x)
            xmat[which] = factor * (2.0 * x - dot3(xparts, tparts))
            tmat[which] = factor * (2.0 * t - dot3(tparts, tparts))
        return carry

    lax.fori_loop(1, steps - 1, step, 0)
    for which in range(2):
        t, x = tmat[which], xmat[which]
        xmat[which] = SCALES[0] * (2.0 * x - dot3(split2(x), split2(t)))

    def correct(i, carry):
        for which in range(2):
            x = xmat[which]
            xparts = split3(x)
            residual = eye - dot6(split3(mat[which]), xparts)
            xmat[which] = x + dot3(xparts, split2(residual))
        return carry

    lax.fori_loop(0, jnp.maximum(steps - 8, 0) + 1, correct, 0)
    for which in range(2):
        high, mid = split2(xmat[which])
        inverse[2 * which] = high
        inverse[2 * which + 1] = mid

    block, chunk = 256, min(tokens, 1024)

    def scores(i, carry):
        here = pl.ds(pl.multiple_of(i * block, block), block)
        qa, qg = query_act[here, :], query_grad[here, :]
        pa = (dot(qa, inverse[0]) + dot(qa, inverse[1])).astype(BF16)
        pg = (dot(qg, inverse[2]) + dot(qg, inverse[3])).astype(BF16)
        total = jnp.zeros((block, columns), F32)
        for first_token in range(0, tokens, chunk):
            these = slice(first_token, first_token + chunk)
            product = dot_nt(pa, act[these, :]) * dot_nt(pg, grad[these, :])
            high, mid = split2(product)
            selector = onehot[:, these]
            total = total + (dot_nt(high, selector) + dot_nt(mid, selector))
        out[here, :] = total * scale
        return carry

    lax.fori_loop(0, query_act.shape[0] // block, scores, 0, unroll=tokens <= 1024)


def gather_spans(payload, size):
    held = [payload]
    bits = [1 << k for k in range(size.bit_length() - 1)]
    for bit in reversed(bits):
        if len(held) >= 16:
            held = [jnp.concatenate(held, axis=0)]
        pairs = [(device, device ^ bit) for device in range(size)]
        held = held + [lax.ppermute(piece, "dp", pairs) for piece in held]
    return held


def local(query_act, query_grad, train_act, train_grad, seq_ids):
    size = lax.axis_size("dp")
    spans, rows, width = train_act.shape
    own = lax.axis_index("dp").astype(BF16)
    ids = jnp.tile(seq_ids.astype(BF16), (1, width // rows)).reshape(spans, 1, width)
    index = jnp.full((spans, 15, width), own, BF16)
    payload = jnp.concatenate([train_act, train_grad, ids, index], axis=1)
    pieces = gather_spans(payload, size)
    tokens, queries, columns = size * spans * rows, query_act.shape[0], size * spans * SEQ_DEV
    scale = 1.0 / (8.0 * math.sqrt(query_act.shape[1] * query_grad.shape[1]))
    vmem = pl.BlockSpec(memory_space=pltpu.VMEM)

    def kernel(*refs):
        influence_kernel(rows, scale, *refs)

    return pl.pallas_call(
        kernel,
        out_shape=jax.ShapeDtypeStruct((queries, columns), F32),
        in_specs=[vmem] * (len(pieces) + 2),
        out_specs=vmem,
        scratch_shapes=[
            pltpu.VMEM((tokens, width), BF16),
            pltpu.VMEM((tokens, width), BF16),
            pltpu.VMEM((columns, tokens), BF16),
            pltpu.VMEM((2, width, width), F32),
            pltpu.VMEM((2, width, width), F32),
            pltpu.VMEM((2, width, width), F32),
            pltpu.VMEM((4, width, width), BF16),
        ],
        compiler_params=pltpu.CompilerParams(vmem_limit_bytes=56 << 20),
    )(*pieces, query_act, query_grad)


def solution(mesh):
    in_specs = (
        P(("grp", "dp"), None),
        P(("grp", "dp"), None),
        P(("grp", "dp"), None, None),
        P(("grp", "dp"), None, None),
        P(("grp", "dp"), None),
    )
    out_specs = P(("grp", "dp"), None)
    return jax.shard_map(local, mesh=mesh, in_specs=in_specs, out_specs=out_specs, check_vma=False)
```

```python
import math

import jax
import jax.numpy as jnp
from jax import lax
from jax.experimental import pallas as pl
from jax.experimental.pallas import tpu as pltpu
from jax.sharding import PartitionSpec as P

SEQ_DEV = 4
DAMPING = 0.1

BF16 = jnp.bfloat16
F32 = jnp.float32


def newton_schedule():
    radius, bounds, scales = 3e-3, [], []
    for _ in range(13):
        before = math.sqrt(2.0 * radius / (1.0 + radius))
        scales.append(2.0 / (2.0 - before * before))
        bounds.append(2.0 * DAMPING / (1.0 - before) - DAMPING)
        radius = before
    return bounds, scales


BOUNDS, SCALES = newton_schedule()


def pick(index, values):
    out = jnp.float32(values[0])
    for position, value in enumerate(values[1:], 2):
        out = jnp.where(index == position, jnp.float32(value), out)
    return out


def split2(x):
    high = x.astype(BF16)
    return high, (x - high.astype(F32)).astype(BF16)


def split3(x):
    high = x.astype(BF16)
    rest = x - high.astype(F32)
    mid = rest.astype(BF16)
    return high, mid, (rest - mid.astype(F32)).astype(BF16)


def dot(a, b):
    return jnp.dot(a, b, preferred_element_type=F32)


def dot3(a, b):
    return dot(a[0], b[0]) + (dot(a[0], b[1]) + dot(a[1], b[0]))


def dot6(a, b):
    small = dot(a[1], b[1]) + (dot(a[0], b[2]) + dot(a[2], b[0]))
    return dot(a[0], b[0]) + ((dot(a[0], b[1]) + dot(a[1], b[0])) + small)


def dot_nt(a, b):
    return lax.dot_general(a, b, (((1,), (1,)), ((), ())), preferred_element_type=F32)


def influence_kernel(rows, scale, *refs):
    n_pieces = len(refs) - 13
    pieces = refs[:n_pieces]
    query_act_hbm, query_grad_hbm, out, query_act, query_grad, act, grad, onehot, mat, tmat, xmat, inverse, arrived = refs[n_pieces:]
    loads = [
        pltpu.make_async_copy(query_act_hbm, query_act, arrived.at[0]),
        pltpu.make_async_copy(query_grad_hbm, query_grad, arrived.at[1]),
    ]
    for load in loads:
        load.start()
    tokens, width = act.shape
    columns = onehot.shape[0]
    lane = lax.broadcasted_iota(jnp.int32, (1, 128), 1)
    column = lax.broadcasted_iota(jnp.int32, (columns, 128), 0)

    spans = [(ref, k) for ref in pieces for k in range(ref.shape[0])]
    labels = []
    for slot, (ref, k) in enumerate(spans):
        act[slot * rows : (slot + 1) * rows, :] = ref[k, 0:rows, :]
        grad[slot * rows : (slot + 1) * rows, :] = ref[k, rows : 2 * rows, :]
        tail = ref[k, 2 * rows : 2 * rows + 8, 0:128].astype(F32)
        labels.append((SEQ_DEV * tail[1:2, :] + tail[0:1, :]).astype(jnp.int32))
    for pair in range(tokens // 128):
        label = jnp.where(lane < rows, labels[2 * pair], labels[2 * pair + 1])
        onehot[:, pair * 128 : (pair + 1) * 128] = (column == label).astype(F32).astype(BF16)

    diagonal = lax.broadcasted_iota(jnp.int32, (width, width), 0) == lax.broadcasted_iota(jnp.int32, (width, width), 1)
    eye = diagonal.astype(F32)
    norm = jnp.float32(0.0)
    for which, features in enumerate((act, grad)):
        flat = features[...]
        covar = lax.dot_general(flat, flat, (((0,), (0,)), ((), ())), preferred_element_type=F32)
        matrix = covar * (1.0 / tokens) + DAMPING * eye
        mat[which] = matrix
        norm = jnp.maximum(norm, jnp.sum(matrix * matrix))

    steps = jnp.int32(2)
    for bound in BOUNDS[1:-1]:
        steps = steps + (norm > bound * bound).astype(jnp.int32)
    start = pick(steps, [2.0 / (DAMPING + bound) for bound in BOUNDS])

    first = pick(steps, SCALES)
    for which in range(2):
        t = start * mat[which]
        parts = split2(t)
        xmat[which] = (first * start) * (2.0 * eye - t)
        tmat[which] = first * (2.0 * t - dot3(parts, parts))

    def step(i, carry):
        factor = pick(steps - i, SCALES)
        for which in range(2):
            t, x = tmat[which], xmat[which]
            tparts, xparts = split2(t), split2(x)
            xmat[which] = factor * (2.0 * x - dot3(xparts, tparts))
            tmat[which] = factor * (2.0 * t - dot3(tparts, tparts))
        return carry

    lax.fori_loop(1, steps - 1, step, 0)
    for which in range(2):
        t, x = tmat[which], xmat[which]
        xmat[which] = SCALES[0] * (2.0 * x - dot3(split2(x), split2(t)))

    def correct(i, carry):
        for which in range(2):
            x = xmat[which]
            xparts = split3(x)
            residual = eye - dot6(split3(mat[which]), xparts)
            xmat[which] = x + dot3(xparts, split2(residual))
        return carry

    lax.fori_loop(0, jnp.maximum(steps - 8, 0) + 1, correct, 0)
    for which in range(2):
        high, mid = split2(xmat[which])
        inverse[2 * which] = high
        inverse[2 * which + 1] = mid

    for load in loads:
        load.wait()
    block, chunk = 256, min(tokens, 1024)

    def scores(i, carry):
        here = pl.ds(pl.multiple_of(i * block, block), block)
        qa, qg = query_act[here, :], query_grad[here, :]
        pa = (dot(qa, inverse[0]) + dot(qa, inverse[1])).astype(BF16)
        pg = (dot(qg, inverse[2]) + dot(qg, inverse[3])).astype(BF16)
        total = jnp.zeros((block, columns), F32)
        for first_token in range(0, tokens, chunk):
            these = slice(first_token, first_token + chunk)
            product = dot_nt(pa, act[these, :]) * dot_nt(pg, grad[these, :])
            high, mid = split2(product)
            selector = onehot[:, these]
            total = total + (dot_nt(high, selector) + dot_nt(mid, selector))
        out[:, here] = (total * scale).T
        return carry

    lax.fori_loop(0, query_act.shape[0] // block, scores, 0, unroll=tokens <= 1024)


def payload_kernel(rows, act, grad, ids, out):
    out[0, 0:rows, :] = act[0]
    out[0, rows : 2 * rows, :] = grad[0]
    index = lax.axis_index("dp").astype(F32)
    label = ids[...].astype(F32)
    label = jnp.broadcast_to(jnp.concatenate([label] * (act.shape[2] // rows), axis=1), (8, act.shape[2]))
    row = lax.broadcasted_iota(jnp.int32, label.shape, 0)
    out[0, 2 * rows :, :] = jnp.where(row == 0, label, index).astype(BF16)


ROUTE_16 = ((0, 8), (0, 4), (0, 2), (1, 4), (1, 2), (2, 2), (5, 4))


def exchange(piece, bit, size):
    return lax.ppermute(piece, "dp", [(device, device ^ bit) for device in range(size)])


def gather_spans(payload, size):
    held = [payload]
    if size == 16:
        for source, bit in ROUTE_16:
            held.append(exchange(held[source], bit, size))
        return held + [exchange(piece, 1, size) for piece in held]
    for bit in reversed([1 << k for k in range(size.bit_length() - 1)]):
        if len(held) >= 16:
            held = [jnp.concatenate(held, axis=0)]
        held = held + [exchange(piece, bit, size) for piece in held]
    return held


def local(query_act, query_grad, train_act, train_grad, seq_ids):
    size = lax.axis_size("dp")
    spans, rows, width = train_act.shape
    vmem = pl.BlockSpec(memory_space=pltpu.VMEM)

    def build(*refs):
        payload_kernel(rows, *refs)

    payload = pl.pallas_call(
        build,
        out_shape=pltpu.VMEM((spans, 2 * rows + 8, width), BF16),
        in_specs=[vmem] * 3,
        out_specs=vmem,
    )(train_act, train_grad, seq_ids)
    pieces = gather_spans(payload, size)
    tokens, queries, columns = size * spans * rows, query_act.shape[0], size * spans * SEQ_DEV
    scale = 1.0 / (8.0 * math.sqrt(query_act.shape[1] * query_grad.shape[1]))

    def kernel(*refs):
        influence_kernel(rows, scale, *refs)

    operands = [pltpu.with_memory_space_constraint(piece, pltpu.VMEM) for piece in pieces]
    scores = pl.pallas_call(
        kernel,
        out_shape=jax.ShapeDtypeStruct((columns, queries), F32),
        in_specs=[vmem] * len(operands) + [pl.BlockSpec(memory_space=pltpu.HBM)] * 2,
        out_specs=vmem,
        scratch_shapes=[
            pltpu.VMEM(query_act.shape, BF16),
            pltpu.VMEM(query_grad.shape, BF16),
            pltpu.VMEM((tokens, width), BF16),
            pltpu.VMEM((tokens, width), BF16),
            pltpu.VMEM((columns, tokens), BF16),
            pltpu.VMEM((2, width, width), F32),
            pltpu.VMEM((2, width, width), F32),
            pltpu.VMEM((2, width, width), F32),
            pltpu.VMEM((4, width, width), BF16),
            pltpu.SemaphoreType.DMA((2,)),
        ],
        compiler_params=pltpu.CompilerParams(vmem_limit_bytes=40 << 20),
    )(*operands, query_act, query_grad)
    return scores.T


def solution(mesh):
    in_specs = (
        P(("grp", "dp"), None),
        P(("grp", "dp"), None),
        P(("grp", "dp"), None, None),
        P(("grp", "dp"), None, None),
        P(("grp", "dp"), None),
    )
    out_specs = P(("grp", "dp"), None)
    return jax.shard_map(local, mesh=mesh, in_specs=in_specs, out_specs=out_specs, check_vma=False)
```

```python
import math

import jax
import jax.numpy as jnp
from jax import lax
from jax.experimental import pallas as pl
from jax.experimental.pallas import tpu as pltpu
from jax.sharding import PartitionSpec as P

SEQ_DEV = 4
DAMPING = 0.1

BF16 = jnp.bfloat16
F32 = jnp.float32


FAST_STEPS = 7


def newton_schedule():
    radius, bounds, scales = 0.02, [], []
    for _ in range(13):
        before = math.sqrt(2.0 * radius / (1.0 + radius))
        scales.append(2.0 / (2.0 - before * before))
        bounds.append(2.0 * DAMPING / (1.0 - before) - DAMPING)
        radius = before
    return bounds, scales


BOUNDS, SCALES = newton_schedule()


def pick(steps, values):
    out = jnp.float32(values[FAST_STEPS - 1])
    for position in range(FAST_STEPS + 1, len(values) + 1):
        out = jnp.where(steps == position, jnp.float32(values[position - 1]), out)
    return out


def split2(x):
    high = x.astype(BF16)
    return high, (x - high.astype(F32)).astype(BF16)


def split3(x):
    high = x.astype(BF16)
    rest = x - high.astype(F32)
    mid = rest.astype(BF16)
    return high, mid, (rest - mid.astype(F32)).astype(BF16)


def dot(a, b):
    return jnp.dot(a, b, preferred_element_type=F32)


def dot3(a, b):
    return dot(a[0], b[0]) + (dot(a[0], b[1]) + dot(a[1], b[0]))


def dot6(a, b):
    small = dot(a[1], b[1]) + (dot(a[0], b[2]) + dot(a[2], b[0]))
    return dot(a[0], b[0]) + ((dot(a[0], b[1]) + dot(a[1], b[0])) + small)


def dot_nt(a, b):
    return lax.dot_general(a, b, (((1,), (1,)), ((), ())), preferred_element_type=F32)


def corrected(matrices, xs, eye):
    xparts = [split3(x) for x in xs]
    residuals = [eye - dot6(split3(matrix), parts) for matrix, parts in zip(matrices, xparts)]
    highs = [residual.astype(BF16) for residual in residuals]
    sums = [split2(residual + dot(high, high)) for residual, high in zip(residuals, highs)]
    return [x + dot3(parts, total) for x, parts, total in zip(xs, xparts, sums)]


def influence_kernel(rows, scale, *refs):
    n_pieces = len(refs) - 13
    pieces = refs[:n_pieces]
    query_act_hbm, query_grad_hbm, out, query_act, query_grad, act, grad, onehot, mat, tmat, xmat, inverse, arrived = refs[n_pieces:]
    loads = [
        pltpu.make_async_copy(query_act_hbm, query_act, arrived.at[0]),
        pltpu.make_async_copy(query_grad_hbm, query_grad, arrived.at[1]),
    ]
    for load in loads:
        load.start()
    tokens, width = act.shape
    columns = onehot.shape[0]
    lane = lax.broadcasted_iota(jnp.int32, (1, 128), 1)
    column = lax.broadcasted_iota(jnp.int32, (columns, 128), 0)

    spans = [(ref, k) for ref in pieces for k in range(ref.shape[0])]
    labels = []
    for slot, (ref, k) in enumerate(spans):
        act[slot * rows : (slot + 1) * rows, :] = ref[k, 0:rows, :]
        grad[slot * rows : (slot + 1) * rows, :] = ref[k, rows : 2 * rows, :]
        tail = ref[k, 2 * rows : 2 * rows + 8, 0:128].astype(F32)
        labels.append((SEQ_DEV * tail[1:2, :] + tail[0:1, :]).astype(jnp.int32))
    for pair in range(tokens // 128):
        label = jnp.where(lane < rows, labels[2 * pair], labels[2 * pair + 1])
        onehot[:, pair * 128 : (pair + 1) * 128] = (column == label).astype(F32).astype(BF16)

    diagonal = lax.broadcasted_iota(jnp.int32, (width, width), 0) == lax.broadcasted_iota(jnp.int32, (width, width), 1)
    eye = diagonal.astype(F32)
    covars = [
        lax.dot_general(flat, flat, (((0,), (0,)), ((), ())), preferred_element_type=F32) for flat in (act[...], grad[...])
    ]
    matrices = [covar * (1.0 / tokens) + DAMPING * eye for covar in covars]
    squares = [dot3(parts, parts) for parts in map(split2, matrices)]
    norm = jnp.maximum(jnp.sum(squares[0] * squares[0]), jnp.sum(squares[1] * squares[1]))

    steps = jnp.int32(FAST_STEPS)
    for bound in BOUNDS[FAST_STEPS - 1 : -1]:
        steps = steps + (norm > 0.99 * bound**4).astype(jnp.int32)

    def first_step(which, square, start, factor):
        t = start * matrices[which]
        return (factor * start) * (2.0 * eye - t), factor * (2.0 * t - (start * start) * square)

    start = 2.0 / (DAMPING + BOUNDS[FAST_STEPS - 1])
    both = [first_step(which, squares[which], start, SCALES[FAST_STEPS - 1]) for which in range(2)]
    for left in range(FAST_STEPS - 1, 0, -1):
        factor = SCALES[left - 1]
        tparts = [split2(t) for _, t in both]
        after = [t for _, t in both]
        if left > 1:
            after = [factor * (2.0 * t - dot3(parts, parts)) for (_, t), parts in zip(both, tparts)]
        both = [
            (factor * (2.0 * x - dot3(split2(x), parts)), t) for (x, _), parts, t in zip(both, tparts, after)
        ]
    for which in range(2):
        xmat[which] = both[which][0]

    @pl.when(steps > FAST_STEPS)
    def _():
        start = pick(steps, [2.0 / (DAMPING + bound) for bound in BOUNDS])
        factor = pick(steps, SCALES)
        for which in range(2):
            parts = split3(matrices[which])
            mat[which] = matrices[which]
            xmat[which], tmat[which] = first_step(which, dot6(parts, parts), start, factor)

        def step(i, carry):
            left = steps - i
            factor = jnp.float32(SCALES[0])
            for position in range(2, len(SCALES) + 1):
                factor = jnp.where(left == position, jnp.float32(SCALES[position - 1]), factor)
            for which in range(2):
                t, x = tmat[which], xmat[which]
                tparts, xparts = split3(t), split3(x)
                xmat[which] = factor * (2.0 * x - dot6(xparts, tparts))
                tmat[which] = factor * (2.0 * t - dot6(tparts, tparts))
            return carry

        lax.fori_loop(1, steps, step, 0)

        for which, x in enumerate(corrected([mat[0], mat[1]], [xmat[0], xmat[1]], eye)):
            xmat[which] = x

    for which, x in enumerate(corrected(matrices, [xmat[0], xmat[1]], eye)):
        inverse[2 * which], inverse[2 * which + 1] = split2(x)

    for load in loads:
        load.wait()
    block, chunk = min(1024, query_act.shape[0]), min(1024, tokens)

    def scores(i, carry):
        here = pl.ds(pl.multiple_of(i * block, block), block)
        qa, qg = query_act[here, :], query_grad[here, :]
        pa = (dot(qa, inverse[0]) + dot(qa, inverse[1])).astype(BF16)
        pg = (dot(qg, inverse[2]) + dot(qg, inverse[3])).astype(BF16)
        total = jnp.zeros((columns, block), F32)
        for first_token in range(0, tokens, chunk):
            these = slice(first_token, first_token + chunk)
            product = dot_nt(act[these, :], pa) * dot_nt(grad[these, :], pg)
            total = total + dot(onehot[:, these], product.astype(BF16))
        out[:, here] = total * scale
        return carry

    lax.fori_loop(0, query_act.shape[0] // block, scores, 0, unroll=tokens <= 1024)


def payload_kernel(rows, act, grad, ids, out):
    out[0, 0:rows, :] = act[0]
    out[0, rows : 2 * rows, :] = grad[0]
    index = lax.axis_index("dp").astype(F32)
    label = ids[...].astype(F32)
    label = jnp.broadcast_to(jnp.concatenate([label] * (act.shape[2] // rows), axis=1), (8, act.shape[2]))
    row = lax.broadcasted_iota(jnp.int32, label.shape, 0)
    out[0, 2 * rows :, :] = jnp.where(row == 0, label, index).astype(BF16)


ROUTE_16 = ((0, 8), (0, 4), (0, 2), (1, 4), (1, 2), (2, 2), (5, 4))


def exchange(piece, bit, size):
    return lax.ppermute(piece, "dp", [(device, device ^ bit) for device in range(size)])


def gather_spans(payload, size):
    held = [payload]
    if size == 16:
        for source, bit in ROUTE_16:
            held.append(exchange(held[source], bit, size))
        return held + [exchange(piece, 1, size) for piece in held]
    for bit in reversed([1 << k for k in range(size.bit_length() - 1)]):
        if len(held) >= 16:
            held = [jnp.concatenate(held, axis=0)]
        held = held + [exchange(piece, bit, size) for piece in held]
    return held


def score_call(pieces, query_act, query_grad, rows):
    spans, queries, width = sum(piece.shape[0] for piece in pieces), query_act.shape[0], query_act.shape[1]
    tokens, columns = spans * rows, spans * SEQ_DEV
    vmem = pl.BlockSpec(memory_space=pltpu.VMEM)
    scale = 1.0 / (8.0 * math.sqrt(query_act.shape[1] * query_grad.shape[1]))

    def kernel(*refs):
        influence_kernel(rows, scale, *refs)

    operands = [pltpu.with_memory_space_constraint(piece, pltpu.VMEM) for piece in pieces]
    scores = pl.pallas_call(
        kernel,
        out_shape=jax.ShapeDtypeStruct((columns, queries), F32),
        in_specs=[vmem] * len(operands) + [pl.BlockSpec(memory_space=pltpu.HBM)] * 2,
        out_specs=vmem,
        scratch_shapes=[
            pltpu.VMEM(query_act.shape, BF16),
            pltpu.VMEM(query_grad.shape, BF16),
            pltpu.VMEM((tokens, width), BF16),
            pltpu.VMEM((tokens, width), BF16),
            pltpu.VMEM((columns, tokens), BF16),
            pltpu.VMEM((2, width, width), F32),
            pltpu.VMEM((2, width, width), F32),
            pltpu.VMEM((2, width, width), F32),
            pltpu.VMEM((4, width, width), BF16),
            pltpu.SemaphoreType.DMA((2,)),
        ],
        compiler_params=pltpu.CompilerParams(vmem_limit_bytes=40 << 20),
    )(*operands, *(pltpu.with_memory_space_constraint(query, pltpu.HBM) for query in (query_act, query_grad)))
    return scores.T


def local(query_act, query_grad, train_act, train_grad, seq_ids):
    size = lax.axis_size("dp")
    spans, rows, width = train_act.shape
    vmem = pl.BlockSpec(memory_space=pltpu.VMEM)

    def build(*refs):
        payload_kernel(rows, *refs)

    payload = pl.pallas_call(
        build,
        out_shape=pltpu.VMEM((spans, 2 * rows + 8, width), BF16),
        in_specs=[vmem] * 3,
        out_specs=vmem,
    )(train_act, train_grad, seq_ids)
    pieces = gather_spans(payload, size)
    return score_call(pieces, query_act, query_grad, rows)


def solution(mesh):
    in_specs = (
        P(("grp", "dp"), None),
        P(("grp", "dp"), None),
        P(("grp", "dp"), None, None),
        P(("grp", "dp"), None, None),
        P(("grp", "dp"), None),
    )
    out_specs = P(("grp", "dp"), None)
    return jax.shard_map(local, mesh=mesh, in_specs=in_specs, out_specs=out_specs, check_vma=False)
```

```python
import math

import jax
import jax.numpy as jnp
from jax import lax
from jax.experimental import pallas as pl
from jax.experimental.pallas import tpu as pltpu
from jax.sharding import PartitionSpec as P

SEQ_DEV = 4
DAMPING = 0.1

BF16 = jnp.bfloat16
F32 = jnp.float32


FAST_STEPS = 7


def newton_schedule():
    radius, bounds, scales = 0.02, [], []
    for _ in range(13):
        before = math.sqrt(2.0 * radius / (1.0 + radius))
        scales.append(2.0 / (2.0 - before * before))
        bounds.append(2.0 * DAMPING / (1.0 - before) - DAMPING)
        radius = before
    return bounds, scales


BOUNDS, SCALES = newton_schedule()


def pick(steps, values):
    out = jnp.float32(values[FAST_STEPS - 1])
    for position in range(FAST_STEPS + 1, len(values) + 1):
        out = jnp.where(steps == position, jnp.float32(values[position - 1]), out)
    return out


def split2(x):
    high = x.astype(BF16)
    return high, (x - high.astype(F32)).astype(BF16)


def split3(x):
    high = x.astype(BF16)
    rest = x - high.astype(F32)
    mid = rest.astype(BF16)
    return high, mid, (rest - mid.astype(F32)).astype(BF16)


def dot(a, b):
    return jnp.dot(a, b, preferred_element_type=F32)


def dot3(a, b):
    return dot(a[0], b[0]) + (dot(a[0], b[1]) + dot(a[1], b[0]))


def dot6(a, b):
    small = dot(a[1], b[1]) + (dot(a[0], b[2]) + dot(a[2], b[0]))
    return dot(a[0], b[0]) + ((dot(a[0], b[1]) + dot(a[1], b[0])) + small)


def dot_nt(a, b):
    return lax.dot_general(a, b, (((1,), (1,)), ((), ())), preferred_element_type=F32)


def corrected(matrices, xs, eye):
    xparts = [split3(x) for x in xs]
    residuals = [eye - dot6(split3(matrix), parts) for matrix, parts in zip(matrices, xparts)]
    highs = [residual.astype(BF16) for residual in residuals]
    sums = [split2(residual + dot(high, high)) for residual, high in zip(residuals, highs)]
    return [x + dot3(parts, total) for x, parts, total in zip(xs, xparts, sums)]


def influence_kernel(rows, scale, *refs):
    n_pieces = len(refs) - 13
    pieces = refs[:n_pieces]
    query_act_hbm, query_grad_hbm, out, query_act, query_grad, act, grad, onehot, mat, tmat, xmat, inverse, arrived = refs[n_pieces:]
    loads = [
        pltpu.make_async_copy(query_act_hbm, query_act, arrived.at[0]),
        pltpu.make_async_copy(query_grad_hbm, query_grad, arrived.at[1]),
    ]
    for load in loads:
        load.start()
    tokens, width = act.shape
    columns = onehot.shape[0]
    lane = lax.broadcasted_iota(jnp.int32, (1, 128), 1)
    column = lax.broadcasted_iota(jnp.int32, (columns, 128), 0)

    spans = [(ref, k) for ref in pieces for k in range(ref.shape[0])]
    labels = []
    for slot, (ref, k) in enumerate(spans):
        act[slot * rows : (slot + 1) * rows, :] = ref[k, 0:rows, :]
        grad[slot * rows : (slot + 1) * rows, :] = ref[k, rows : 2 * rows, :]
        tail = ref[k, 2 * rows : 2 * rows + 8, 0:128].astype(F32)
        labels.append((SEQ_DEV * tail[1:2, :] + tail[0:1, :]).astype(jnp.int32))
    for pair in range(tokens // 128):
        label = jnp.where(lane < rows, labels[2 * pair], labels[2 * pair + 1])
        onehot[:, pair * 128 : (pair + 1) * 128] = (column == label).astype(F32).astype(BF16)

    diagonal = lax.broadcasted_iota(jnp.int32, (width, width), 0) == lax.broadcasted_iota(jnp.int32, (width, width), 1)
    eye = diagonal.astype(F32)
    covars = [
        lax.dot_general(flat, flat, (((0,), (0,)), ((), ())), preferred_element_type=F32) for flat in (act[...], grad[...])
    ]
    matrices = [covar * (1.0 / tokens) + DAMPING * eye for covar in covars]
    squares = [dot3(parts, parts) for parts in map(split2, matrices)]
    norm = jnp.maximum(jnp.sum(squares[0] * squares[0]), jnp.sum(squares[1] * squares[1]))

    steps = jnp.int32(FAST_STEPS)
    for bound in BOUNDS[FAST_STEPS - 1 : -1]:
        steps = steps + (norm > 0.99 * bound**4).astype(jnp.int32)

    def first_step(which, square, start, factor):
        t = start * matrices[which]
        return (factor * start) * (2.0 * eye - t), factor * (2.0 * t - (start * start) * square)

    start = 2.0 / (DAMPING + BOUNDS[FAST_STEPS - 1])
    both = [first_step(which, squares[which], start, SCALES[FAST_STEPS - 1]) for which in range(2)]
    for left in range(FAST_STEPS - 1, 0, -1):
        factor = SCALES[left - 1]
        tparts = [split2(t) for _, t in both]
        after = [t for _, t in both]
        if left > 1:
            after = [factor * (2.0 * t - dot3(parts, parts)) for (_, t), parts in zip(both, tparts)]
        both = [
            (factor * (2.0 * x - dot3(split2(x), parts)), t) for (x, _), parts, t in zip(both, tparts, after)
        ]
    for which in range(2):
        xmat[which] = both[which][0]

    @pl.when(steps > FAST_STEPS)
    def _():
        start = pick(steps, [2.0 / (DAMPING + bound) for bound in BOUNDS])
        factor = pick(steps, SCALES)
        for which in range(2):
            parts = split3(matrices[which])
            mat[which] = matrices[which]
            xmat[which], tmat[which] = first_step(which, dot6(parts, parts), start, factor)

        def step(i, carry):
            left = steps - i
            factor = jnp.float32(SCALES[0])
            for position in range(2, len(SCALES) + 1):
                factor = jnp.where(left == position, jnp.float32(SCALES[position - 1]), factor)
            for which in range(2):
                t, x = tmat[which], xmat[which]
                tparts, xparts = split3(t), split3(x)
                xmat[which] = factor * (2.0 * x - dot6(xparts, tparts))
                tmat[which] = factor * (2.0 * t - dot6(tparts, tparts))
            return carry

        lax.fori_loop(1, steps, step, 0)

        for which, x in enumerate(corrected([mat[0], mat[1]], [xmat[0], xmat[1]], eye)):
            xmat[which] = x

    for which, x in enumerate(corrected(matrices, [xmat[0], xmat[1]], eye)):
        inverse[2 * which], inverse[2 * which + 1] = split2(x)

    for load in loads:
        load.wait()
    block, chunk = min(1024, query_act.shape[0]), min(1024, tokens)

    def scores(i, carry):
        here = pl.ds(pl.multiple_of(i * block, block), block)
        qa, qg = query_act[here, :], query_grad[here, :]
        pa = (dot(qa, inverse[0]) + dot(qa, inverse[1])).astype(BF16)
        pg = (dot(qg, inverse[2]) + dot(qg, inverse[3])).astype(BF16)
        total = jnp.zeros((columns, block), F32)
        for first_token in range(0, tokens, chunk):
            these = slice(first_token, first_token + chunk)
            product = dot_nt(act[these, :], pa) * dot_nt(grad[these, :], pg)
            total = total + dot(onehot[:, these], product.astype(BF16))
        out[:, here] = total * scale
        return carry

    lax.fori_loop(0, query_act.shape[0] // block, scores, 0, unroll=tokens <= 1024)


def payload_kernel(rows, act, grad, ids, out):
    out[0, 0:rows, :] = act[0]
    out[0, rows : 2 * rows, :] = grad[0]
    index = lax.axis_index("dp").astype(F32)
    label = ids[...].astype(F32)
    label = jnp.broadcast_to(jnp.concatenate([label] * (act.shape[2] // rows), axis=1), (8, act.shape[2]))
    row = lax.broadcasted_iota(jnp.int32, label.shape, 0)
    out[0, 2 * rows :, :] = jnp.where(row == 0, label, index).astype(BF16)


ROUTE_16 = (
    ((0, 2), (0, 4), (0, 8), (3, 4), (3, 2), (2, 2), (3, 6))
    + ((7, 1), (6, 1), (5, 1), (4, 1), (1, 1), (2, 1), (3, 1), (0, 1))
)


def exchange(piece, bits, size):
    return lax.ppermute(piece, "dp", [(device, device ^ bits) for device in range(size)])


def gather_spans(payload, size):
    held = [payload]
    if size == 16:
        for source, bits in ROUTE_16:
            held.append(exchange(held[source], bits, size))
        return held
    for bit in reversed([1 << k for k in range(size.bit_length() - 1)]):
        if len(held) >= 16:
            held = [jnp.concatenate(held, axis=0)]
        held = held + [exchange(piece, bit, size) for piece in held]
    return held


def score_call(pieces, query_act, query_grad, rows):
    spans, queries, width = sum(piece.shape[0] for piece in pieces), query_act.shape[0], query_act.shape[1]
    tokens, columns = spans * rows, spans * SEQ_DEV
    vmem = pl.BlockSpec(memory_space=pltpu.VMEM)
    scale = 1.0 / (8.0 * math.sqrt(query_act.shape[1] * query_grad.shape[1]))

    def kernel(*refs):
        influence_kernel(rows, scale, *refs)

    operands = [pltpu.with_memory_space_constraint(piece, pltpu.VMEM) for piece in pieces]
    scores = pl.pallas_call(
        kernel,
        out_shape=jax.ShapeDtypeStruct((columns, queries), F32),
        in_specs=[vmem] * len(operands) + [pl.BlockSpec(memory_space=pltpu.HBM)] * 2,
        out_specs=vmem,
        scratch_shapes=[
            pltpu.VMEM(query_act.shape, BF16),
            pltpu.VMEM(query_grad.shape, BF16),
            pltpu.VMEM((tokens, width), BF16),
            pltpu.VMEM((tokens, width), BF16),
            pltpu.VMEM((columns, tokens), BF16),
            pltpu.VMEM((2, width, width), F32),
            pltpu.VMEM((2, width, width), F32),
            pltpu.VMEM((2, width, width), F32),
            pltpu.VMEM((4, width, width), BF16),
            pltpu.SemaphoreType.DMA((2,)),
        ],
        compiler_params=pltpu.CompilerParams(vmem_limit_bytes=40 << 20),
    )(*operands, *(pltpu.with_memory_space_constraint(query, pltpu.HBM) for query in (query_act, query_grad)))
    return scores.T


def local(query_act, query_grad, train_act, train_grad, seq_ids):
    size = lax.axis_size("dp")
    spans, rows, width = train_act.shape
    vmem = pl.BlockSpec(memory_space=pltpu.VMEM)

    def build(*refs):
        payload_kernel(rows, *refs)

    payload = pl.pallas_call(
        build,
        out_shape=pltpu.VMEM((spans, 2 * rows + 8, width), BF16),
        in_specs=[vmem] * 3,
        out_specs=vmem,
    )(train_act, train_grad, seq_ids)
    pieces = gather_spans(payload, size)
    return score_call(pieces, query_act, query_grad, rows)


def solution(mesh):
    in_specs = (
        P(("grp", "dp"), None),
        P(("grp", "dp"), None),
        P(("grp", "dp"), None, None),
        P(("grp", "dp"), None, None),
        P(("grp", "dp"), None),
    )
    out_specs = P(("grp", "dp"), None)
    return jax.shard_map(local, mesh=mesh, in_specs=in_specs, out_specs=out_specs, check_vma=False)
```

```python
import math

import jax
import jax.numpy as jnp
from jax import lax
from jax.experimental import pallas as pl
from jax.experimental.pallas import tpu as pltpu
from jax.sharding import PartitionSpec as P

SEQ_DEV = 4
DAMPING = 0.1

BF16 = jnp.bfloat16
F32 = jnp.float32


FAST_STEPS = 7


def newton_schedule():
    radius, bounds, scales = 0.02, [], []
    for _ in range(13):
        before = math.sqrt(2.0 * radius / (1.0 + radius))
        scales.append(2.0 / (2.0 - before * before))
        bounds.append(2.0 * DAMPING / (1.0 - before) - DAMPING)
        radius = before
    return bounds, scales


BOUNDS, SCALES = newton_schedule()


def pick(steps, values):
    out = jnp.float32(values[FAST_STEPS - 1])
    for position in range(FAST_STEPS + 1, len(values) + 1):
        out = jnp.where(steps == position, jnp.float32(values[position - 1]), out)
    return out


def split2(x):
    high = x.astype(BF16)
    return high, (x - high.astype(F32)).astype(BF16)


def split3(x):
    high = x.astype(BF16)
    rest = x - high.astype(F32)
    mid = rest.astype(BF16)
    return high, mid, (rest - mid.astype(F32)).astype(BF16)


def dot(a, b):
    return jnp.dot(a, b, preferred_element_type=F32)


def dot3(a, b):
    return dot(a[0], b[0]) + (dot(a[0], b[1]) + dot(a[1], b[0]))


def dot6(a, b):
    small = dot(a[1], b[1]) + (dot(a[0], b[2]) + dot(a[2], b[0]))
    return dot(a[0], b[0]) + ((dot(a[0], b[1]) + dot(a[1], b[0])) + small)


def dot_nt(a, b):
    return lax.dot_general(a, b, (((1,), (1,)), ((), ())), preferred_element_type=F32)


def corrected(matrices, xs, eye):
    xparts = [split3(x) for x in xs]
    residuals = [eye - dot6(split3(matrix), parts) for matrix, parts in zip(matrices, xparts)]
    highs = [residual.astype(BF16) for residual in residuals]
    sums = [split2(residual + dot(high, high)) for residual, high in zip(residuals, highs)]
    return [x + dot3(parts, total) for x, parts, total in zip(xs, xparts, sums)]


def influence_kernel(rows, scale, *refs):
    n_pieces = len(refs) - 13
    pieces = refs[:n_pieces]
    query_act_hbm, query_grad_hbm, out, query_act, query_grad, act, grad, onehot, mat, tmat, xmat, inverse, arrived = refs[n_pieces:]
    loads = [
        pltpu.make_async_copy(query_act_hbm, query_act, arrived.at[0]),
        pltpu.make_async_copy(query_grad_hbm, query_grad, arrived.at[1]),
    ]
    for load in loads:
        load.start()
    tokens, width = act.shape
    columns = onehot.shape[0]
    lane = lax.broadcasted_iota(jnp.int32, (1, 128), 1)
    column = lax.broadcasted_iota(jnp.int32, (columns, 128), 0)

    spans = [(ref, k) for ref in pieces for k in range(ref.shape[0])]
    labels = []
    for slot, (ref, k) in enumerate(spans):
        act[slot * rows : (slot + 1) * rows, :] = ref[k, 0:rows, :]
        grad[slot * rows : (slot + 1) * rows, :] = ref[k, rows : 2 * rows, :]
        tail = ref[k, 2 * rows : 2 * rows + 8, 0:128].astype(F32)
        labels.append((SEQ_DEV * tail[1:2, :] + tail[0:1, :]).astype(jnp.int32))
    for pair in range(tokens // 128):
        label = jnp.where(lane < rows, labels[2 * pair], labels[2 * pair + 1])
        onehot[:, pair * 128 : (pair + 1) * 128] = (column == label).astype(F32).astype(BF16)

    diagonal = lax.broadcasted_iota(jnp.int32, (width, width), 0) == lax.broadcasted_iota(jnp.int32, (width, width), 1)
    eye = diagonal.astype(F32)
    covars = [
        lax.dot_general(flat, flat, (((0,), (0,)), ((), ())), preferred_element_type=F32) for flat in (act[...], grad[...])
    ]
    matrices = [covar * (1.0 / tokens) + DAMPING * eye for covar in covars]
    squares = [dot3(parts, parts) for parts in map(split2, matrices)]
    norm = jnp.maximum(jnp.sum(squares[0] * squares[0]), jnp.sum(squares[1] * squares[1]))

    steps = jnp.int32(FAST_STEPS)
    for bound in BOUNDS[FAST_STEPS - 1 : -1]:
        steps = steps + (norm > 0.99 * bound**4).astype(jnp.int32)

    def first_step(which, square, start, factor):
        t = start * matrices[which]
        return (factor * start) * (2.0 * eye - t), factor * (2.0 * t - (start * start) * square)

    start = 2.0 / (DAMPING + BOUNDS[FAST_STEPS - 1])
    both = [first_step(which, squares[which], start, SCALES[FAST_STEPS - 1]) for which in range(2)]
    for left in range(FAST_STEPS - 1, 0, -1):
        factor = SCALES[left - 1]
        tparts = [split2(t) for _, t in both]
        after = [t for _, t in both]
        if left > 1:
            after = [factor * (2.0 * t - dot3(parts, parts)) for (_, t), parts in zip(both, tparts)]
        both = [
            (factor * (2.0 * x - dot3(split2(x), parts)), t) for (x, _), parts, t in zip(both, tparts, after)
        ]
    for which, x in enumerate(corrected(matrices, [x for x, _ in both], eye)):
        inverse[2 * which], inverse[2 * which + 1] = split2(x)

    for load in loads:
        load.wait()

    @pl.when(steps > FAST_STEPS)
    def _():
        start = pick(steps, [2.0 / (DAMPING + bound) for bound in BOUNDS])
        factor = pick(steps, SCALES)
        for which in range(2):
            parts = split3(matrices[which])
            mat[which] = matrices[which]
            xmat[which], tmat[which] = first_step(which, dot6(parts, parts), start, factor)

        def step(i, carry):
            left = steps - i
            factor = jnp.float32(SCALES[0])
            for position in range(2, len(SCALES) + 1):
                factor = jnp.where(left == position, jnp.float32(SCALES[position - 1]), factor)
            for which in range(2):
                t, x = tmat[which], xmat[which]
                tparts, xparts = split3(t), split3(x)
                xmat[which] = factor * (2.0 * x - dot6(xparts, tparts))
                tmat[which] = factor * (2.0 * t - dot6(tparts, tparts))
            return carry

        lax.fori_loop(1, steps, step, 0)

        for which, x in enumerate(corrected([mat[0], mat[1]], [xmat[0], xmat[1]], eye)):
            xmat[which] = x
        for which, x in enumerate(corrected([mat[0], mat[1]], [xmat[0], xmat[1]], eye)):
            inverse[2 * which], inverse[2 * which + 1] = split2(x)


    block, chunk = min(1024, query_act.shape[0]), min(1024, tokens)

    def scores(i, carry):
        here = pl.ds(pl.multiple_of(i * block, block), block)
        qa, qg = query_act[here, :], query_grad[here, :]
        pa = (dot(qa, inverse[0]) + dot(qa, inverse[1])).astype(BF16)
        pg = (dot(qg, inverse[2]) + dot(qg, inverse[3])).astype(BF16)
        total = jnp.zeros((columns, block), F32)
        for first_token in range(0, tokens, chunk):
            these = slice(first_token, first_token + chunk)
            product = dot_nt(act[these, :], pa) * dot_nt(grad[these, :], pg)
            total = total + dot(onehot[:, these], product.astype(BF16))
        out[:, here] = total * scale
        return carry

    lax.fori_loop(0, query_act.shape[0] // block, scores, 0, unroll=tokens <= 1024)


def payload_kernel(rows, act, grad, ids, out):
    out[0, 0:rows, :] = act[0]
    out[0, rows : 2 * rows, :] = grad[0]
    index = lax.axis_index("dp").astype(F32)
    label = ids[...].astype(F32)
    label = jnp.broadcast_to(jnp.concatenate([label] * (act.shape[2] // rows), axis=1), (8, act.shape[2]))
    row = lax.broadcasted_iota(jnp.int32, label.shape, 0)
    out[0, 2 * rows :, :] = jnp.where(row == 0, label, index).astype(BF16)


ROUTE_16 = (
    ((0, 6), (0, 2), (0, 4), (0, 8), (4, 2), (4, 4), (4, 6))
    + ((7, 1), (1, 1), (5, 1), (6, 1), (2, 1), (3, 1), (4, 1), (0, 1))
)


def exchange(piece, bits, size):
    return lax.ppermute(piece, "dp", [(device, device ^ bits) for device in range(size)])


def gather_spans(payload, size):
    held = [payload]
    if size == 16:
        for source, bits in ROUTE_16:
            held.append(exchange(held[source], bits, size))
        return held
    for bit in reversed([1 << k for k in range(size.bit_length() - 1)]):
        if len(held) >= 16:
            held = [jnp.concatenate(held, axis=0)]
        held = held + [exchange(piece, bit, size) for piece in held]
    return held


def score_call(pieces, query_act, query_grad, rows):
    spans, queries, width = sum(piece.shape[0] for piece in pieces), query_act.shape[0], query_act.shape[1]
    tokens, columns = spans * rows, spans * SEQ_DEV
    vmem = pl.BlockSpec(memory_space=pltpu.VMEM)
    scale = 1.0 / (8.0 * math.sqrt(query_act.shape[1] * query_grad.shape[1]))

    def kernel(*refs):
        influence_kernel(rows, scale, *refs)

    operands = [pltpu.with_memory_space_constraint(piece, pltpu.VMEM) for piece in pieces]
    scores = pl.pallas_call(
        kernel,
        out_shape=jax.ShapeDtypeStruct((columns, queries), F32),
        in_specs=[vmem] * len(operands) + [pl.BlockSpec(memory_space=pltpu.HBM)] * 2,
        out_specs=vmem,
        scratch_shapes=[
            pltpu.VMEM(query_act.shape, BF16),
            pltpu.VMEM(query_grad.shape, BF16),
            pltpu.VMEM((tokens, width), BF16),
            pltpu.VMEM((tokens, width), BF16),
            pltpu.VMEM((columns, tokens), BF16),
            pltpu.VMEM((2, width, width), F32),
            pltpu.VMEM((2, width, width), F32),
            pltpu.VMEM((2, width, width), F32),
            pltpu.VMEM((4, width, width), BF16),
            pltpu.SemaphoreType.DMA((2,)),
        ],
        compiler_params=pltpu.CompilerParams(vmem_limit_bytes=40 << 20),
    )(*operands, *(pltpu.with_memory_space_constraint(query, pltpu.HBM) for query in (query_act, query_grad)))
    return scores.T


def local(query_act, query_grad, train_act, train_grad, seq_ids):
    size = lax.axis_size("dp")
    spans, rows, width = train_act.shape
    vmem = pl.BlockSpec(memory_space=pltpu.VMEM)

    def build(*refs):
        payload_kernel(rows, *refs)

    payload = pl.pallas_call(
        build,
        out_shape=pltpu.VMEM((spans, 2 * rows + 8, width), BF16),
        in_specs=[vmem] * 3,
        out_specs=vmem,
    )(train_act, train_grad, seq_ids)
    pieces = gather_spans(payload, size)
    return score_call(pieces, query_act, query_grad, rows)


def solution(mesh):
    in_specs = (
        P(("grp", "dp"), None),
        P(("grp", "dp"), None),
        P(("grp", "dp"), None, None),
        P(("grp", "dp"), None, None),
        P(("grp", "dp"), None),
    )
    out_specs = P(("grp", "dp"), None)
    return jax.shard_map(local, mesh=mesh, in_specs=in_specs, out_specs=out_specs, check_vma=False)
```

```python
import math

import jax
import jax.numpy as jnp
from jax import lax
from jax.experimental import pallas as pl
from jax.experimental.pallas import tpu as pltpu
from jax.sharding import PartitionSpec as P

SEQ_DEV = 4
DAMPING = 0.1

BF16 = jnp.bfloat16
F32 = jnp.float32


FAST_STEPS = 7


def newton_schedule():
    radius, bounds, scales = 0.02, [], []
    for _ in range(13):
        before = math.sqrt(2.0 * radius / (1.0 + radius))
        scales.append(2.0 / (2.0 - before * before))
        bounds.append(2.0 * DAMPING / (1.0 - before) - DAMPING)
        radius = before
    return bounds, scales


BOUNDS, SCALES = newton_schedule()


def pick(steps, values):
    out = jnp.float32(values[FAST_STEPS - 1])
    for position in range(FAST_STEPS + 1, len(values) + 1):
        out = jnp.where(steps == position, jnp.float32(values[position - 1]), out)
    return out


def split2(x):
    high = x.astype(BF16)
    return high, (x - high.astype(F32)).astype(BF16)


def split3(x):
    high = x.astype(BF16)
    rest = x - high.astype(F32)
    mid = rest.astype(BF16)
    return high, mid, (rest - mid.astype(F32)).astype(BF16)


def dot(a, b):
    return jnp.dot(a, b, preferred_element_type=F32)


def dot3(a, b):
    return dot(a[0], b[0]) + (dot(a[0], b[1]) + dot(a[1], b[0]))


def dot6(a, b):
    small = dot(a[1], b[1]) + (dot(a[0], b[2]) + dot(a[2], b[0]))
    return dot(a[0], b[0]) + ((dot(a[0], b[1]) + dot(a[1], b[0])) + small)


def dot_nt(a, b):
    return lax.dot_general(a, b, (((1,), (1,)), ((), ())), preferred_element_type=F32)


def corrected(matrices, xs, eye):
    xparts = [split3(x) for x in xs]
    residuals = [eye - dot6(split3(matrix), parts) for matrix, parts in zip(matrices, xparts)]
    highs = [residual.astype(BF16) for residual in residuals]
    sums = [split2(residual + dot(high, high)) for residual, high in zip(residuals, highs)]
    return [x + dot3(parts, total) for x, parts, total in zip(xs, xparts, sums)]


def influence_kernel(rows, scale, *refs):
    n_pieces = len(refs) - 13
    pieces = refs[:n_pieces]
    query_act_hbm, query_grad_hbm, out, query_act, query_grad, act, grad, onehot, mat, tmat, xmat, inverse, arrived = refs[n_pieces:]
    loads = [
        pltpu.make_async_copy(query_act_hbm, query_act, arrived.at[0]),
        pltpu.make_async_copy(query_grad_hbm, query_grad, arrived.at[1]),
    ]
    for load in loads:
        load.start()
    tokens, width = act.shape
    columns = onehot.shape[0]
    lane = lax.broadcasted_iota(jnp.int32, (1, 128), 1)
    column = lax.broadcasted_iota(jnp.int32, (columns, 128), 0)

    spans = [(ref, k) for ref in pieces for k in range(ref.shape[0])]
    labels = []
    for slot, (ref, k) in enumerate(spans):
        act[slot * rows : (slot + 1) * rows, :] = ref[k, 0:rows, :]
        grad[slot * rows : (slot + 1) * rows, :] = ref[k, rows : 2 * rows, :]
        tail = ref[k, 2 * rows : 2 * rows + 8, 0:128].astype(F32)
        labels.append((SEQ_DEV * tail[1:2, :] + tail[0:1, :]).astype(jnp.int32))
    for pair in range(tokens // 128):
        label = jnp.where(lane < rows, labels[2 * pair], labels[2 * pair + 1])
        onehot[:, pair * 128 : (pair + 1) * 128] = (column == label).astype(F32).astype(BF16)

    diagonal = lax.broadcasted_iota(jnp.int32, (width, width), 0) == lax.broadcasted_iota(jnp.int32, (width, width), 1)
    eye = diagonal.astype(F32)
    covars = [
        lax.dot_general(flat, flat, (((0,), (0,)), ((), ())), preferred_element_type=F32) for flat in (act[...], grad[...])
    ]
    matrices = [covar * (1.0 / tokens) + DAMPING * eye for covar in covars]
    squares = [dot3(parts, parts) for parts in map(split2, matrices)]
    norm = jnp.maximum(jnp.sum(squares[0] * squares[0]), jnp.sum(squares[1] * squares[1]))

    steps = jnp.int32(FAST_STEPS)
    for bound in BOUNDS[FAST_STEPS - 1 : -1]:
        steps = steps + (norm > 0.99 * bound**4).astype(jnp.int32)

    def first_step(which, square, start, factor):
        t = start * matrices[which]
        return (factor * start) * (2.0 * eye - t), factor * (2.0 * t - (start * start) * square)

    start = 2.0 / (DAMPING + BOUNDS[FAST_STEPS - 1])
    both = [first_step(which, squares[which], start, SCALES[FAST_STEPS - 1]) for which in range(2)]
    for left in range(FAST_STEPS - 1, 0, -1):
        factor = SCALES[left - 1]
        tparts = [split2(t) for _, t in both]
        after = [t for _, t in both]
        if left > 1:
            after = [factor * (2.0 * t - dot3(parts, parts)) for (_, t), parts in zip(both, tparts)]
        both = [
            (factor * (2.0 * x - dot3(split2(x), parts)), t) for (x, _), parts, t in zip(both, tparts, after)
        ]
    for which, x in enumerate(corrected(matrices, [x for x, _ in both], eye)):
        inverse[2 * which], inverse[2 * which + 1] = split2(x)

    for load in loads:
        load.wait()

    @pl.when(steps > FAST_STEPS)
    def _():
        start = pick(steps, [2.0 / (DAMPING + bound) for bound in BOUNDS])
        factor = pick(steps, SCALES)
        for which in range(2):
            parts = split3(matrices[which])
            mat[which] = matrices[which]
            xmat[which], tmat[which] = first_step(which, dot6(parts, parts), start, factor)

        def step(i, carry):
            left = steps - i
            factor = jnp.float32(SCALES[0])
            for position in range(2, len(SCALES) + 1):
                factor = jnp.where(left == position, jnp.float32(SCALES[position - 1]), factor)
            for which in range(2):
                t, x = tmat[which], xmat[which]
                tparts, xparts = split3(t), split3(x)
                xmat[which] = factor * (2.0 * x - dot6(xparts, tparts))
                tmat[which] = factor * (2.0 * t - dot6(tparts, tparts))
            return carry

        lax.fori_loop(1, steps, step, 0)

        for which, x in enumerate(corrected([mat[0], mat[1]], [xmat[0], xmat[1]], eye)):
            xmat[which] = x
        for which, x in enumerate(corrected([mat[0], mat[1]], [xmat[0], xmat[1]], eye)):
            inverse[2 * which], inverse[2 * which + 1] = split2(x)


    block, chunk = min(1024, query_act.shape[0]), min(1024, tokens)

    def scores(i, carry):
        here = pl.ds(pl.multiple_of(i * block, block), block)
        qa, qg = query_act[here, :], query_grad[here, :]
        pa = (dot(qa, inverse[0]) + dot(qa, inverse[1])).astype(BF16)
        pg = (dot(qg, inverse[2]) + dot(qg, inverse[3])).astype(BF16)
        total = jnp.zeros((columns, block), F32)
        for first_token in range(0, tokens, chunk):
            these = slice(first_token, first_token + chunk)
            product = dot_nt(act[these, :], pa) * dot_nt(grad[these, :], pg)
            total = total + dot(onehot[:, these], product.astype(BF16))
        out[:, here] = total * scale
        return carry

    lax.fori_loop(0, query_act.shape[0] // block, scores, 0, unroll=tokens <= 1024)


def payload_kernel(rows, act, grad, ids, out):
    out[0, 0:rows, :] = act[0]
    out[0, rows : 2 * rows, :] = grad[0]
    index = lax.axis_index("dp").astype(F32)
    label = ids[...].astype(F32)
    label = jnp.broadcast_to(jnp.concatenate([label] * (act.shape[2] // rows), axis=1), (8, act.shape[2]))
    row = lax.broadcasted_iota(jnp.int32, label.shape, 0)
    out[0, 2 * rows :, :] = jnp.where(row == 0, label, index).astype(BF16)


ROUTE_16 = (
    ((0, 6), (0, 2), (0, 4), (0, 8), (4, 2), (4, 4), (4, 6))
    + ((5, 1), (1, 1), (7, 1), (6, 1), (2, 1), (3, 1), (4, 1), (0, 1))
)


def exchange(piece, bits, size):
    return lax.ppermute(piece, "dp", [(device, device ^ bits) for device in range(size)])


def gather_spans(payload, size):
    held = [payload]
    if size == 16:
        for source, bits in ROUTE_16:
            held.append(exchange(held[source], bits, size))
        return held
    for bit in reversed([1 << k for k in range(size.bit_length() - 1)]):
        if len(held) >= 16:
            held = [jnp.concatenate(held, axis=0)]
        held = held + [exchange(piece, bit, size) for piece in held]
    return held


def score_call(pieces, query_act, query_grad, rows):
    spans, queries, width = sum(piece.shape[0] for piece in pieces), query_act.shape[0], query_act.shape[1]
    tokens, columns = spans * rows, spans * SEQ_DEV
    vmem = pl.BlockSpec(memory_space=pltpu.VMEM)
    scale = 1.0 / (8.0 * math.sqrt(query_act.shape[1] * query_grad.shape[1]))

    def kernel(*refs):
        influence_kernel(rows, scale, *refs)

    operands = [pltpu.with_memory_space_constraint(piece, pltpu.VMEM) for piece in pieces]
    scores = pl.pallas_call(
        kernel,
        out_shape=jax.ShapeDtypeStruct((columns, queries), F32),
        in_specs=[vmem] * len(operands) + [pl.BlockSpec(memory_space=pltpu.HBM)] * 2,
        out_specs=vmem,
        scratch_shapes=[
            pltpu.VMEM(query_act.shape, BF16),
            pltpu.VMEM(query_grad.shape, BF16),
            pltpu.VMEM((tokens, width), BF16),
            pltpu.VMEM((tokens, width), BF16),
            pltpu.VMEM((columns, tokens), BF16),
            pltpu.VMEM((2, width, width), F32),
            pltpu.VMEM((2, width, width), F32),
            pltpu.VMEM((2, width, width), F32),
            pltpu.VMEM((4, width, width), BF16),
            pltpu.SemaphoreType.DMA((2,)),
        ],
        compiler_params=pltpu.CompilerParams(vmem_limit_bytes=40 << 20),
    )(*operands, *(pltpu.with_memory_space_constraint(query, pltpu.HBM) for query in (query_act, query_grad)))
    return scores.T


def local(query_act, query_grad, train_act, train_grad, seq_ids):
    size = lax.axis_size("dp")
    spans, rows, width = train_act.shape
    vmem = pl.BlockSpec(memory_space=pltpu.VMEM)

    def build(*refs):
        payload_kernel(rows, *refs)

    payload = pl.pallas_call(
        build,
        out_shape=pltpu.VMEM((spans, 2 * rows + 8, width), BF16),
        in_specs=[vmem] * 3,
        out_specs=vmem,
    )(train_act, train_grad, seq_ids)
    pieces = gather_spans(payload, size)
    return score_call(pieces, query_act, query_grad, rows)


def solution(mesh):
    in_specs = (
        P(("grp", "dp"), None),
        P(("grp", "dp"), None),
        P(("grp", "dp"), None, None),
        P(("grp", "dp"), None, None),
        P(("grp", "dp"), None),
    )
    out_specs = P(("grp", "dp"), None)
    return jax.shard_map(local, mesh=mesh, in_specs=in_specs, out_specs=out_specs, check_vma=False)
```

```python
import math

import jax
import jax.numpy as jnp
from jax import lax
from jax.experimental import pallas as pl
from jax.experimental.pallas import tpu as pltpu
from jax.sharding import PartitionSpec as P

SEQ_DEV = 4
DAMPING = 0.1

BF16 = jnp.bfloat16
F32 = jnp.float32


FAST_STEPS = 7


def newton_schedule():
    radius, bounds, scales = 0.02, [], []
    for _ in range(13):
        before = math.sqrt(2.0 * radius / (1.0 + radius))
        scales.append(2.0 / (2.0 - before * before))
        bounds.append(2.0 * DAMPING / (1.0 - before) - DAMPING)
        radius = before
    return bounds, scales


BOUNDS, SCALES = newton_schedule()


def pick(steps, values):
    out = jnp.float32(values[FAST_STEPS - 1])
    for position in range(FAST_STEPS + 1, len(values) + 1):
        out = jnp.where(steps == position, jnp.float32(values[position - 1]), out)
    return out


def split2(x):
    high = x.astype(BF16)
    return high, (x - high.astype(F32)).astype(BF16)


def split3(x):
    high = x.astype(BF16)
    rest = x - high.astype(F32)
    mid = rest.astype(BF16)
    return high, mid, (rest - mid.astype(F32)).astype(BF16)


def dot(a, b):
    return jnp.dot(a, b, preferred_element_type=F32)


def dot3(a, b):
    return dot(a[0], b[0]) + (dot(a[0], b[1]) + dot(a[1], b[0]))


def dot6(a, b):
    small = dot(a[1], b[1]) + (dot(a[0], b[2]) + dot(a[2], b[0]))
    return dot(a[0], b[0]) + ((dot(a[0], b[1]) + dot(a[1], b[0])) + small)


def dot_nt(a, b):
    return lax.dot_general(a, b, (((1,), (1,)), ((), ())), preferred_element_type=F32)


def corrected(matrices, xs, eye):
    xparts = [split3(x) for x in xs]
    residuals = [eye - dot6(split3(matrix), parts) for matrix, parts in zip(matrices, xparts)]
    highs = [residual.astype(BF16) for residual in residuals]
    sums = [split2(residual + dot(high, high)) for residual, high in zip(residuals, highs)]
    return [x + dot3(parts, total) for x, parts, total in zip(xs, xparts, sums)]


def influence_kernel(rows, scale, *refs):
    n_pieces = len(refs) - 13
    pieces = refs[:n_pieces]
    query_act_hbm, query_grad_hbm, out, query_act, query_grad, act, grad, onehot, mat, tmat, xmat, inverse, arrived = refs[n_pieces:]
    loads = [
        pltpu.make_async_copy(query_act_hbm, query_act, arrived.at[0]),
        pltpu.make_async_copy(query_grad_hbm, query_grad, arrived.at[1]),
    ]
    for load in loads:
        load.start()
    tokens, width = act.shape
    columns = onehot.shape[0]
    lane = lax.broadcasted_iota(jnp.int32, (1, 128), 1)
    column = lax.broadcasted_iota(jnp.int32, (columns, 128), 0)

    spans = [(ref, k) for ref in pieces for k in range(ref.shape[0])]
    labels = []
    for slot, (ref, k) in enumerate(spans):
        act[slot * rows : (slot + 1) * rows, :] = ref[k, 0:rows, :]
        grad[slot * rows : (slot + 1) * rows, :] = ref[k, rows : 2 * rows, :]
        tail = ref[k, 2 * rows : 2 * rows + 8, 0:128].astype(F32)
        labels.append((SEQ_DEV * tail[1:2, :] + tail[0:1, :]).astype(jnp.int32))
    for pair in range(tokens // 128):
        label = jnp.where(lane < rows, labels[2 * pair], labels[2 * pair + 1])
        onehot[:, pair * 128 : (pair + 1) * 128] = (column == label).astype(F32).astype(BF16)

    diagonal = lax.broadcasted_iota(jnp.int32, (width, width), 0) == lax.broadcasted_iota(jnp.int32, (width, width), 1)
    eye = diagonal.astype(F32)
    covars = [
        lax.dot_general(flat, flat, (((0,), (0,)), ((), ())), preferred_element_type=F32) for flat in (act[...], grad[...])
    ]
    matrices = [covar * (1.0 / tokens) + DAMPING * eye for covar in covars]
    squares = [dot3(parts, parts) for parts in map(split2, matrices)]

    def first_step(which, square, start, factor):
        t = start * matrices[which]
        return (factor * start) * (2.0 * eye - t), factor * (2.0 * t - (start * start) * square)

    start = 2.0 / (DAMPING + BOUNDS[FAST_STEPS - 1])
    both = [first_step(which, squares[which], start, SCALES[FAST_STEPS - 1]) for which in range(2)]
    for left in range(FAST_STEPS - 1, 0, -1):
        factor = SCALES[left - 1]
        tparts = [split2(t) for _, t in both]
        after = [t for _, t in both]
        if left > 1:
            after = [factor * (2.0 * t - dot3(parts, parts)) for (_, t), parts in zip(both, tparts)]
        both = [
            (factor * (2.0 * x - dot3(split2(x), parts)), t) for (x, _), parts, t in zip(both, tparts, after)
        ]
    for which, x in enumerate(corrected(matrices, [x for x, _ in both], eye)):
        inverse[2 * which], inverse[2 * which + 1] = split2(x)

    norm = jnp.maximum(jnp.sum(squares[0] * squares[0]), jnp.sum(squares[1] * squares[1]))

    steps = jnp.int32(FAST_STEPS)
    for bound in BOUNDS[FAST_STEPS - 1 : -1]:
        steps = steps + (norm > 0.99 * bound**4).astype(jnp.int32)

    for load in loads:
        load.wait()

    @pl.when(steps > FAST_STEPS)
    def _():
        start = pick(steps, [2.0 / (DAMPING + bound) for bound in BOUNDS])
        factor = pick(steps, SCALES)
        for which in range(2):
            parts = split3(matrices[which])
            mat[which] = matrices[which]
            xmat[which], tmat[which] = first_step(which, dot6(parts, parts), start, factor)

        def step(i, carry):
            left = steps - i
            factor = jnp.float32(SCALES[0])
            for position in range(2, len(SCALES) + 1):
                factor = jnp.where(left == position, jnp.float32(SCALES[position - 1]), factor)
            for which in range(2):
                t, x = tmat[which], xmat[which]
                tparts, xparts = split3(t), split3(x)
                xmat[which] = factor * (2.0 * x - dot6(xparts, tparts))
                tmat[which] = factor * (2.0 * t - dot6(tparts, tparts))
            return carry

        lax.fori_loop(1, steps, step, 0)

        for which, x in enumerate(corrected([mat[0], mat[1]], [xmat[0], xmat[1]], eye)):
            xmat[which] = x
        for which, x in enumerate(corrected([mat[0], mat[1]], [xmat[0], xmat[1]], eye)):
            inverse[2 * which], inverse[2 * which + 1] = split2(x)


    block, chunk = min(1024, query_act.shape[0]), min(1024, tokens)

    def scores(i, carry):
        here = pl.ds(pl.multiple_of(i * block, block), block)
        qa, qg = query_act[here, :], query_grad[here, :]
        pa = (dot(qa, inverse[0]) + dot(qa, inverse[1])).astype(BF16)
        pg = (dot(qg, inverse[2]) + dot(qg, inverse[3])).astype(BF16)
        total = jnp.zeros((columns, block), F32)
        for first_token in range(0, tokens, chunk):
            these = slice(first_token, first_token + chunk)
            product = dot_nt(act[these, :], pa) * dot_nt(grad[these, :], pg)
            total = total + dot(onehot[:, these], product.astype(BF16))
        out[:, here] = total * scale
        return carry

    lax.fori_loop(0, query_act.shape[0] // block, scores, 0, unroll=tokens <= 1024)


def payload_kernel(rows, act, grad, ids, out):
    out[0, 0:rows, :] = act[0]
    out[0, rows : 2 * rows, :] = grad[0]
    index = lax.axis_index("dp").astype(F32)
    label = ids[...].astype(F32)
    label = jnp.broadcast_to(jnp.concatenate([label] * (act.shape[2] // rows), axis=1), (8, act.shape[2]))
    row = lax.broadcasted_iota(jnp.int32, label.shape, 0)
    out[0, 2 * rows :, :] = jnp.where(row == 0, label, index).astype(BF16)


ROUTE_16 = (
    ((0, 6), (0, 2), (0, 4), (0, 8), (4, 2), (4, 4), (4, 6))
    + ((7, 1), (1, 1), (5, 1), (6, 1), (2, 1), (3, 1), (4, 1), (0, 1))
)


def exchange(piece, bits, size):
    return lax.ppermute(piece, "dp", [(device, device ^ bits) for device in range(size)])


def gather_spans(payload, size):
    held = [payload]
    if size == 16:
        for source, bits in ROUTE_16:
            held.append(exchange(held[source], bits, size))
        return held
    for bit in reversed([1 << k for k in range(size.bit_length() - 1)]):
        if len(held) >= 16:
            held = [jnp.concatenate(held, axis=0)]
        held = held + [exchange(piece, bit, size) for piece in held]
    return held


def score_call(pieces, query_act, query_grad, rows):
    spans, queries, width = sum(piece.shape[0] for piece in pieces), query_act.shape[0], query_act.shape[1]
    tokens, columns = spans * rows, spans * SEQ_DEV
    vmem = pl.BlockSpec(memory_space=pltpu.VMEM)
    scale = 1.0 / (8.0 * math.sqrt(query_act.shape[1] * query_grad.shape[1]))

    def kernel(*refs):
        influence_kernel(rows, scale, *refs)

    operands = [pltpu.with_memory_space_constraint(piece, pltpu.VMEM) for piece in pieces]
    scores = pl.pallas_call(
        kernel,
        out_shape=jax.ShapeDtypeStruct((columns, queries), F32),
        in_specs=[vmem] * len(operands) + [pl.BlockSpec(memory_space=pltpu.HBM)] * 2,
        out_specs=vmem,
        scratch_shapes=[
            pltpu.VMEM(query_act.shape, BF16),
            pltpu.VMEM(query_grad.shape, BF16),
            pltpu.VMEM((tokens, width), BF16),
            pltpu.VMEM((tokens, width), BF16),
            pltpu.VMEM((columns, tokens), BF16),
            pltpu.VMEM((2, width, width), F32),
            pltpu.VMEM((2, width, width), F32),
            pltpu.VMEM((2, width, width), F32),
            pltpu.VMEM((4, width, width), BF16),
            pltpu.SemaphoreType.DMA((2,)),
        ],
        compiler_params=pltpu.CompilerParams(vmem_limit_bytes=40 << 20),
    )(*operands, *(pltpu.with_memory_space_constraint(query, pltpu.HBM) for query in (query_act, query_grad)))
    return scores.T


def local(query_act, query_grad, train_act, train_grad, seq_ids):
    size = lax.axis_size("dp")
    spans, rows, width = train_act.shape
    vmem = pl.BlockSpec(memory_space=pltpu.VMEM)

    def build(*refs):
        payload_kernel(rows, *refs)

    payload = pl.pallas_call(
        build,
        out_shape=pltpu.VMEM((spans, 2 * rows + 8, width), BF16),
        in_specs=[vmem] * 3,
        out_specs=vmem,
    )(train_act, train_grad, seq_ids)
    pieces = gather_spans(payload, size)
    return score_call(pieces, query_act, query_grad, rows)


def solution(mesh):
    in_specs = (
        P(("grp", "dp"), None),
        P(("grp", "dp"), None),
        P(("grp", "dp"), None, None),
        P(("grp", "dp"), None, None),
        P(("grp", "dp"), None),
    )
    out_specs = P(("grp", "dp"), None)
    return jax.shard_map(local, mesh=mesh, in_specs=in_specs, out_specs=out_specs, check_vma=False)
```
